256 devices in a mesh: batch: 32 (over z, x), tensor: 8 (over y, core).
Axes of the slice: x: 4, y: 4, z: 8, core: 2. Of those that a mesh axis runs over, the one named last changes fastest.
Arguments:
- tokens: bfloat16 [8192, 4096], P(('batch', 'tensor')), may hold values from -6 to 6
- norm_gain: float32 [4096], replicated, may hold values from 0.1 to 1.9
- w_query: bfloat16 [4096, 4096], P(None, 'tensor'), may hold values from -0.09375 to 0.09375
- w_key: bfloat16 [4096, 1024], P(None, 'tensor'), may hold values from -0.25 to 0.25
- w_value: bfloat16 [4096, 1024], P(None, 'tensor'), may hold values from -0.09375 to 0.09375
- w_out: bfloat16 [4096, 4096], P('tensor'), may hold values from -0.25 to 0.25
- prefix_keys: bfloat16 [16384, 1024], P('batch', 'tensor'), may hold values from -6 to 6
- prefix_values: bfloat16 [16384, 1024], P('batch', 'tensor'), may hold values from -6 to 6
- cache_keys: bfloat16 [147456, 1024], P('batch', 'tensor'), may hold values from -160 to 160
- cache_values: bfloat16 [147456, 1024], P('batch', 'tensor'), may hold values from -6 to 6
- cache_lengths: int32 [128], replicated, may hold values from 128 to 2048, as said below
- prefix_used: int32 [128], P('batch'), may hold values from 4096 to 16384
- parents: int32 [128, 64], P('batch'), may hold values from 0 to 62, as said below
- accepted_index: int32 [128, 8], P('batch'), may hold values from 0 to 63, as said below
Outputs:
- mixed_output: bfloat16 [8192, 4096], P(('batch', 'tensor'))
- accepted_keys: bfloat16 [128, 8, 1024], P('batch', None, 'tensor')
- accepted_values: bfloat16 [128, 8, 1024], P('batch', None, 'tensor')
The draws below stay inside these ranges and needn't reach their ends.
Inputs may be any that keep to these rules, and one draw needn't show every extreme that they name: `cache_lengths`: within each aligned group of 4 requests at most 2 have more than 256 cached tokens; in the first group exactly that many do, and some request has exactly 2048. parents[r, 0] = 0; for i >= 1, parents[r, i] lies between max(0, i - 8) and i - 1. `accepted_index`: each row lists 8 tree positions, each the parent of the next, ending at a position of 32 or more; where the root is reached the row repeats 0 at its front.
All inputs are finite; a program needn't handle non-finite values.
Results may differ from the reference program's by a relative error of at most 0.015.
The reference program's roundings to bfloat16 on the way count: a program that leaves them out, or rounds other values in their place, can miss the bound.
Values may be sent and summed in bfloat16 or wider, within the bound.
A program may use at most 192 MiB of HBM per device.

```python
import jax
import jax.numpy as jnp
from jax import lax

D = 4096
HD = 128
QH = 32
KVH = 8
TREE = 64
PATH = 8
SHORT = 256
LONG = 2048
REQ_DEV = 4
REQUESTS = 128
TOKENS = 8192
CACHE_DEV = 4608
CACHE_ALL = 147456
PREFIX = 16384
N_TENSOR = 8


def draw_tree(key):
    position = jnp.arange(TREE, dtype=jnp.int32)
    lowest = jnp.maximum(position - 8, 0)
    highest = jnp.maximum(position, 1)
    return jax.random.randint(key, (REQUESTS, TREE), lowest[None, :], highest[None, :], dtype=jnp.int32)


def draw_parents(key, part):
    return draw_tree(jax.random.fold_in(key, 11))


def draw_accepted_index(key, part):
    parents = draw_tree(jax.random.fold_in(key, 11))
    current = jax.random.randint(jax.random.fold_in(key, 12), (REQUESTS,), TREE // 2, TREE, dtype=jnp.int32)
    chain_nodes = [current]
    for repeat in range(PATH - 1):
        current = jnp.take_along_axis(parents, current[:, None], axis=1)[:, 0]
        chain_nodes.append(current)
    return jnp.stack(chain_nodes[::-1], axis=1).astype(jnp.int32)


def draw_cache_lengths(key, part):
    groups = REQUESTS // REQ_DEV
    most_long = REQ_DEV // 2
    long_count = jax.random.randint(jax.random.fold_in(key, 21), (groups,), 0, most_long + 1, dtype=jnp.int32)
    long_count = long_count.at[0].set(most_long)
    ranking = jax.vmap(lambda subkey: jax.random.permutation(subkey, REQ_DEV))(jax.random.split(jax.random.fold_in(key, 22), groups))
    long_value = jax.random.randint(jax.random.fold_in(key, 23), (groups, REQ_DEV), 3 * LONG // 4, LONG + 1, dtype=jnp.int32)
    short_value = jax.random.randint(jax.random.fold_in(key, 24), (groups, REQ_DEV), SHORT // 2, SHORT + 1, dtype=jnp.int32)
    lengths = jnp.where(ranking < long_count[:, None], long_value, short_value)
    group_index = jnp.arange(groups, dtype=jnp.int32)[:, None]
    lengths = jnp.where((group_index == 0) & (ranking == 0), LONG, lengths)
    return lengths.reshape(REQUESTS).astype(jnp.int32)


def draw_cache_keys(key, part):
    shape = (CACHE_ALL, KVH * HD)
    return jnp.clip(jax.random.normal(jax.random.fold_in(key, 33), shape, jnp.float32), -5.0, 5.0).astype(jnp.bfloat16)


def set_ends(values, stream_key, least, high):
    index_at = [jax.random.randint(jax.random.fold_in(stream_key, axis), (), 0, length) for axis, length in enumerate(values.shape)]
    main_axis = values.shape.index(max(values.shape))
    beside = index_at[:main_axis] + [(index_at[main_axis] + 1) % values.shape[main_axis]] + index_at[main_axis + 1:]
    return values.at[tuple(index_at)].set(least).at[tuple(beside)].set(high)


def block_scale(own_key, extent, cuts, least, top_value):
    gain = 1.0
    for dim, shards_of in cuts:
        heights = jax.random.uniform(jax.random.fold_in(jax.random.fold_in(own_key, 6), dim), (shards_of,), jnp.float32, least / len(cuts), top_value / len(cuts))
        gain = gain * jnp.repeat(jnp.exp(heights), extent[dim] // shards_of).reshape((-1,) + (1,) * (len(extent) - 1 - dim))
    return gain


def noise(rng, shape, spread, most, cuts=(), kind=jnp.bfloat16):
    values = spread * jax.random.normal(rng, shape, jnp.float32)
    if cuts:
        values = values * block_scale(rng, shape, cuts, -0.22, 0.18)
    return jnp.clip(values, -most, most).astype(kind)


def setup_inputs(seed: int = 0) -> dict:
    seeds = jax.random.split(jax.random.key(seed), 15)
    return {
        "tokens": noise(seeds[0], (TOKENS, D), 1.0, 6.0, ((0, 256),)),
        "norm_gain": jnp.clip(1.0 + 0.18 * jax.random.normal(seeds[1], (D,), jnp.float32), 0.1, 1.9),
        "w_query": noise(seeds[2], (D, QH * HD), D ** -0.5, 0.09375, ((1, 8),)),
        "w_key": noise(seeds[3], (D, KVH * HD), (D // 9) ** -0.5, 0.25, ((1, 8),)),
        "w_value": noise(seeds[4], (D, KVH * HD), D ** -0.5, 0.09375, ((1, 8),)),
        "w_out": noise(seeds[5], (QH * HD, D), (QH * HD // 9) ** -0.5, 0.25, ((0, 8),)),
        "prefix_keys": noise(seeds[6], (PREFIX, KVH * HD), 1.0, 6.0, ((0, 32), (1, 8))),
        "prefix_values": noise(seeds[7], (PREFIX, KVH * HD), 1.0, 6.0, ((0, 32), (1, 8))),
        "cache_keys": draw_cache_keys(jax.random.fold_in(seeds[14], 71), 0),
        "cache_values": noise(seeds[9], (CACHE_ALL, KVH * HD), 1.0, 6.0, ((0, 32), (1, 8))),
        "cache_lengths": draw_cache_lengths(jax.random.fold_in(seeds[14], 71), 0),
        "prefix_used": set_ends(jax.random.randint(seeds[11], (REQUESTS,), PREFIX // 4, PREFIX + 1), jax.random.fold_in(seeds[11], 1), PREFIX // 4, PREFIX).astype(jnp.int32),
        "parents": draw_parents(jax.random.fold_in(seeds[14], 71), 0),
        "accepted_index": draw_accepted_index(jax.random.fold_in(seeds[14], 71), 0),
    }


NEG_FILL = -1e+30
HIGHEST = lax.Precision.HIGHEST

def rms_normed(tokens, norm_gain):
    values = tokens.astype(jnp.float32)
    factor = lax.rsqrt(lax.optimization_barrier(jnp.mean(values * values, axis=-1, keepdims=True)) + 1e-05)
    return (values * factor * norm_gain).astype(jnp.bfloat16)

def ancestor_table(parents):
    node_count = parents.shape[-1]
    column = jnp.arange(node_count, dtype=jnp.int32)
    linked = (parents[..., None] == column).astype(jnp.float32)
    itself = (column[:, None] == column[None, :]).astype(jnp.float32)
    ancestry = jnp.minimum(linked + itself, 1.0)
    for repeat in range(node_count.bit_length()):
        ancestry = jnp.minimum(jnp.einsum('rij,rjk->rik', ancestry, ancestry, precision=HIGHEST), 1.0)
    return ancestry

def rotate(values, positions):
    half_width = values.shape[-1] // 2
    frequency = 10000.0 ** (-jnp.arange(half_width, dtype=jnp.float32) / half_width)
    angles = positions.astype(jnp.float32)[:, None] * frequency[None, :]
    cosine = jnp.cos(angles)[:, None, :]
    sine_table = jnp.sin(angles)[:, None, :]
    first_half = values[..., :half_width]
    second_half = values[..., half_width:]
    return jnp.concatenate([first_half * cosine - second_half * sine_table, second_half * cosine + first_half * sine_table], axis=-1)

def reference(tokens, norm_gain, w_query, w_key, w_value, w_out, prefix_keys, prefix_values, cache_keys, cache_values, cache_lengths, prefix_used, parents, accepted_index):
    group_size = QH // KVH
    normed = rms_normed(tokens, norm_gain)
    query_raw = jnp.dot(normed, w_query, preferred_element_type=jnp.float32)
    key_raw = jnp.dot(normed, w_key, preferred_element_type=jnp.float32)
    value_raw = jnp.dot(normed, w_value, preferred_element_type=jnp.float32)
    ancestry = ancestor_table(parents)
    tree_depth = (lax.optimization_barrier(jnp.sum(ancestry, axis=-1)) - 1.0).astype(jnp.int32)
    position = ((prefix_used + cache_lengths)[:, None] + tree_depth).reshape(TOKENS)
    queries = rotate(query_raw.reshape(TOKENS, QH, HD), position).astype(jnp.bfloat16)
    queries = queries.reshape(REQUESTS, TREE, KVH, group_size, HD)
    new_keys = rotate(key_raw.reshape(TOKENS, KVH, HD), position).astype(jnp.bfloat16)
    new_keys = new_keys.reshape(REQUESTS, TREE, KVH * HD)
    new_values = value_raw.astype(jnp.bfloat16).reshape(REQUESTS, TREE, KVH * HD)
    accepted_keys = jnp.take_along_axis(new_keys, accepted_index[:, :, None], axis=1)
    accepted_values = jnp.take_along_axis(new_values, accepted_index[:, :, None], axis=1)
    per_group = cache_lengths.reshape(REQUESTS // REQ_DEV, REQ_DEV)
    group_base = (jnp.arange(REQUESTS // REQ_DEV, dtype=jnp.int32) * CACHE_DEV)[:, None]
    offset = (jnp.cumsum(per_group, axis=1) - per_group + group_base).reshape(REQUESTS).astype(jnp.int32)
    padding = jnp.zeros((LONG, KVH * HD), jnp.bfloat16)
    padded_keys = jnp.concatenate([cache_keys, padding], axis=0)
    padded_values = jnp.concatenate([cache_values, padding], axis=0)
    shared_keys = prefix_keys.reshape(PREFIX, KVH, HD)
    shared_values = prefix_values.reshape(PREFIX, KVH, HD)
    prefix_slots = jnp.arange(PREFIX, dtype=jnp.int32)
    cache_slots = jnp.arange(LONG, dtype=jnp.int32)

    def one_request(request_items):
        request_query, request_keys, request_values, request_table, request_offset, length, used = request_items
        corner = (request_offset.astype(jnp.int32), jnp.zeros((), jnp.int32))
        cached_keys = lax.dynamic_slice(padded_keys, corner, (LONG, KVH * HD)).reshape(LONG, KVH, HD)
        cached_values = lax.dynamic_slice(padded_values, corner, (LONG, KVH * HD)).reshape(LONG, KVH, HD)
        all_keys = jnp.concatenate([shared_keys, cached_keys, request_keys.reshape(TREE, KVH, HD)], axis=0).astype(jnp.float32)
        all_values = jnp.concatenate([shared_values, cached_values, request_values.reshape(TREE, KVH, HD)], axis=0).astype(jnp.float32)
        visible = jnp.concatenate([jnp.broadcast_to((prefix_slots < used)[None, :], (TREE, PREFIX)), jnp.broadcast_to((cache_slots < length)[None, :], (TREE, LONG)), request_table > 0.5], axis=1)
        score = jnp.einsum('ihgd,khd->hgik', request_query.astype(jnp.float32), all_keys) * HD ** (-0.5)
        masked = jnp.where(visible[None, None], score, NEG_FILL)
        largest = lax.optimization_barrier(jnp.max(masked, axis=-1, keepdims=True))
        weights = jnp.where(visible[None, None], jnp.exp(masked - largest), 0.0)
        denominator = lax.optimization_barrier(jnp.sum(weights, axis=-1))
        rounded_weights = lax.optimization_barrier(weights.astype(jnp.bfloat16)).astype(jnp.float32)
        numerator = jnp.einsum('hgik,khd->ihgd', rounded_weights, all_values)
        result = numerator / jnp.transpose(denominator, (2, 0, 1))[..., None]
        return result.astype(jnp.bfloat16).reshape(TREE, QH * HD)
    attended = lax.map(one_request, (queries, new_keys, new_values, ancestry, offset, cache_lengths, prefix_used))
    attended = attended.reshape(TOKENS, QH * HD)
    share = QH * HD // N_TENSOR
    summed = jnp.zeros((TOKENS, D), jnp.float32)
    for group in range(N_TENSOR):
        partial_value = jnp.dot(attended[:, group * share:(group + 1) * share], w_out[group * share:(group + 1) * share], preferred_element_type=jnp.float32)
        summed = summed + lax.optimization_barrier(partial_value.astype(jnp.bfloat16)).astype(jnp.float32)
    return (summed.astype(jnp.bfloat16), accepted_keys, accepted_values)
```

```python
import jax
import jax.numpy as jnp
from jax import lax
from jax.experimental import pallas as pl
from jax.experimental.pallas import tpu as pltpu
from jax.sharding import PartitionSpec as P

HD = 128
TREE = 64
GROUP = 4
REQ = 4
NX = 4
NZ = 8
NY = 4
BLOCK = 512
CACHE_BLOCK = 512
NEG_FILL = -1e30
LOG2E = 1.4426950408889634
SCALE2 = HD ** (-0.5) * LOG2E
MESH = pl.DeviceIdType.MESH
ORDER = (0, 1, 3, 2)
F32 = jnp.float32
BF16 = jnp.bfloat16


def place():
    batch = lax.axis_index("batch")
    tensor = lax.axis_index("tensor")
    z, x = lax.div(batch, NX), lax.rem(batch, NX)
    y, core = lax.div(tensor, 2), lax.rem(tensor, 2)
    return batch, tensor, z, x, y, core


def remote(src, dst, send, recv, device):
    return pltpu.make_async_remote_copy(
        src_ref=src, dst_ref=dst, send_sem=send, recv_sem=recv, device_id=device, device_id_type=MESH
    )


def greet(devices):
    barrier = pltpu.get_barrier_semaphore()
    for device in devices:
        pl.semaphore_signal(barrier, inc=1, device_id=device, device_id_type=MESH)
    pl.semaphore_wait(barrier, len(devices))


def project_kernel(
    used_s, len_s, par, gain, freq, tok, wq, wk, wv, pk, pv,
    q_all, k_all, v_all, new_k, new_v, anc, used_all,
    tokb, wb, normb, qb, nkb, nvb, ancb, usedb, cosb, sinb, kvb,
    tok_s, tok_r, kv_s, kv_r, q_s, q_r, us_s, us_r, loc,
):
    batch, me, z, x, y, core = place()
    yp = lax.rem(y + 1, NY) * 2 + core
    ym = lax.rem(y + 3, NY) * 2 + core
    y2 = lax.rem(y + 2, NY) * 2 + core
    other = y * 2 + 1 - core
    oyp = lax.rem(y + 1, NY) * 2 + 1 - core
    oym = lax.rem(y + 3, NY) * 2 + 1 - core
    oy2 = lax.rem(y + 2, NY) * 2 + 1 - core
    zp = lax.rem(z + 1, NZ) * NX + x
    zm = lax.rem(z + NZ - 1, NZ) * NX + x
    x_up, x_down, x_far = lax.rem(x + 1, NX), lax.rem(x + 3, NX), lax.rem(x + 2, NX)
    xp, xm, xf = z * NX + x_up, z * NX + x_down, z * NX + x_far
    top, low = pl.ds(0, 16), pl.ds(16, 16)

    loads = [
        pltpu.make_async_copy(tok, tokb.at[me], loc.at[0]),
        pltpu.make_async_copy(wq, wb.at[:, pl.ds(0, 512)], loc.at[1]),
        pltpu.make_async_copy(wk, wb.at[:, pl.ds(512, 128)], loc.at[2]),
        pltpu.make_async_copy(wv, wb.at[:, pl.ds(640, 128)], loc.at[3]),
        pltpu.make_async_copy(pk, kvb.at[0], loc.at[4]),
        pltpu.make_async_copy(pv, kvb.at[1], loc.at[5]),
    ]
    for load in loads:
        load.start()

    lane = lax.broadcasted_iota(jnp.int32, (8, HD), 1)
    used_row = jnp.zeros((8, HD), jnp.int32)
    for r in range(REQ):
        used_row = jnp.where(lane == r, used_s[r], used_row)
    usedb[...] = used_row

    greet([(batch, yp), (batch, ym), (batch, other), (zp, me), (zm, me), (xp, me), (xm, me), (xf, me)])

    def tok_copy(index, src, slot, rows, target):
        dst = tokb.at[slot] if rows is None else tokb.at[slot, rows]
        return remote(src, dst, tok_s.at[index], tok_r.at[index], (batch, target))

    def tok_land(index, slot, rows):
        dst = tokb.at[slot] if rows is None else tokb.at[slot, rows]
        return remote(dst, dst, tok_s.at[index], tok_r.at[index], (batch, other))

    sends = []

    def go(copy):
        copy.start()
        sends.append(copy)

    def kv_parts(direction, chunk):
        hop = chunk // 2
        is_key = (chunk + direction) % 2 == 0
        gathered = k_all if is_key else v_all
        own = pk if is_key else pv
        return hop, gathered, own

    def kv_send(direction, chunk):
        hop, gathered, own = kv_parts(direction, chunk)
        if direction == 0:
            block, target = lax.rem(z + NZ - hop, NZ), zp
        else:
            block, target = lax.rem(z + hop, NZ), zm
        src = own if hop == 0 else gathered.at[block]
        go(remote(src, gathered.at[block], kv_s.at[direction, chunk], kv_r.at[direction, chunk], (target, me)))

    def kv_land(direction, chunk):
        hop, gathered, own = kv_parts(direction, chunk)
        if direction == 0:
            block = lax.rem(z + NZ - 1 - hop, NZ)
        else:
            block = lax.rem(z + 1 + hop, NZ)
        dst = gathered.at[block]
        remote(dst, dst, kv_s.at[direction, chunk], kv_r.at[direction, chunk], (zp, me)).wait_recv()

    def kv_step(chunk):
        for direction in range(2):
            kv_land(direction, chunk - 2)
            kv_send(direction, chunk)

    go(tok_copy(0, tok.at[top], me, top, yp))
    go(tok_copy(2, tok.at[low], me, low, ym))
    for direction in range(2):
        kv_send(direction, 0)
    go(tok_copy(4, tok, me, None, other))
    go(tok_copy(1, tok.at[low], me, low, yp))
    go(tok_copy(3, tok.at[top], me, top, ym))
    for direction in range(2):
        kv_send(direction, 1)
    for index, (target, device) in enumerate(((xp, x_up), (xm, x_down), (xf, x_far))):
        go(remote(usedb, used_all.at[x], us_s.at[index], us_r.at[index], (target, me)))

    row = lax.broadcasted_iota(jnp.int32, (TREE, TREE), 0)
    col = lax.broadcasted_iota(jnp.int32, (TREE, TREE), 1)
    tables = []
    for r in range(REQ):
        hit = (row == par[pl.ds(r, 1), :]) | (row == col)
        tables.append(jnp.where(hit, 1.0, 0.0))
    for repeat in range(6):
        tables = [
            jnp.minimum(jnp.dot(a.astype(BF16), a.astype(BF16), preferred_element_type=F32), 1.0) for a in tables
        ]
    upper = lax.broadcasted_iota(jnp.int32, (TREE, HD), 1) < HD // 2
    for r in range(REQ):
        table = tables[r].T
        ancb[pl.ds(r * TREE, TREE), :] = table
        depth = jnp.sum(table, axis=1, keepdims=True) - 1.0
        base = (used_s[r] + len_s[batch * REQ + r]).astype(F32)
        angles = (depth + base) * freq[...]
        cosb[r] = jnp.cos(angles)
        sine = jnp.sin(angles)
        sinb[r] = jnp.where(upper, -sine, sine)

    for load in loads:
        load.wait()
    stores = [
        pltpu.make_async_copy(kvb.at[0], k_all.at[z], loc.at[4]),
        pltpu.make_async_copy(kvb.at[1], v_all.at[z], loc.at[5]),
        pltpu.make_async_copy(usedb, used_all.at[x], loc.at[6]),
        pltpu.make_async_copy(ancb, anc, loc.at[7]),
    ]
    for store in stores:
        store.start()

    def request_of(j):
        return lax.rem(y + ORDER[j], NY)

    def project(j):
        r = request_of(j)
        for half in range(2):
            values = tokb[2 * r + half].astype(F32)
            factor = lax.rsqrt(jnp.mean(values * values, axis=-1, keepdims=True) + 1e-05)
            normb[pl.ds(half * 32, 32), :] = (values * factor * gain[...]).astype(BF16)

        def step(k, total):
            rows = pl.ds(pl.multiple_of(k * 512, 512), 512)
            return total + jnp.dot(normb[:, rows], wb[rows, :], preferred_element_type=F32)

        total = lax.fori_loop(0, 8, step, jnp.zeros((TREE, 768), F32))
        cosine, sine = cosb[r], sinb[r]

        def turn(head):
            return (head * cosine + pltpu.roll(head, HD // 2, 1) * sine).astype(BF16)

        for g in range(GROUP):
            qb[r, pl.ds(g * TREE, TREE), :] = turn(total[:, g * HD : (g + 1) * HD])
        nkb[r] = turn(total[:, 512:640])
        nvb[r] = total[:, 640:768].astype(BF16)
        go(remote(qb.at[r], q_all.at[x, r], q_s.at[0, j], q_r.at[0, j], (xp, me)))
        go(remote(qb.at[r], q_all.at[x, r], q_s.at[1, j], q_r.at[1, j], (xm, me)))

    def q_relay(j):
        r = request_of(j)
        lower = q_all.at[x_down, r]
        remote(lower, lower, q_s.at[0, j], q_r.at[0, j], (xp, me)).wait_recv()
        part = q_all.at[x_down, r, pl.ds(0, 128)]
        go(remote(part, part, q_s.at[2, j], q_r.at[2, j], (xp, me)))
        higher = q_all.at[x_up, r]
        remote(higher, higher, q_s.at[1, j], q_r.at[1, j], (xm, me)).wait_recv()
        part = q_all.at[x_up, r, pl.ds(128, 128)]
        go(remote(part, part, q_s.at[3, j], q_r.at[3, j], (xm, me)))

    tok_land(0, ym, top).wait_recv()
    go(tok_copy(5, tokb.at[ym, top], ym, top, yp))
    tok_land(2, yp, low).wait_recv()
    go(tok_copy(6, tokb.at[yp, low], yp, low, ym))
    kv_step(2)
    tok_land(4, other, None).wait_recv()
    project(0)
    tok_land(3, yp, top).wait_recv()
    go(tok_copy(8, tokb.at[yp], yp, None, other))
    tok_land(1, ym, low).wait_recv()
    go(tok_copy(7, tokb.at[ym], ym, None, other))
    kv_step(3)
    tok_land(8, oyp, None).wait_recv()
    project(1)
    q_relay(0)
    tok_land(5, y2, top).wait_recv()
    go(tok_copy(9, tokb.at[y2, top], y2, top, other))
    tok_land(6, y2, low).wait_recv()
    go(tok_copy(10, tokb.at[y2, low], y2, low, other))
    kv_step(4)
    tok_land(7, oym, None).wait_recv()
    project(2)
    q_relay(1)
    kv_step(5)
    tok_land(9, oy2, top).wait_recv()
    tok_land(10, oy2, low).wait_recv()
    project(3)
    out_copies = [
        pltpu.make_async_copy(qb, q_all.at[x], loc.at[0]),
        pltpu.make_async_copy(nkb, new_k, loc.at[1]),
        pltpu.make_async_copy(nvb, new_v, loc.at[2]),
    ]
    for copy in out_copies:
        copy.start()
    kv_step(6)
    q_relay(2)
    q_relay(3)
    for j in range(REQ):
        r = request_of(j)
        part = q_all.at[x_far, r, pl.ds(0, 128)]
        remote(part, part, q_s.at[2, j], q_r.at[2, j], (xp, me)).wait_recv()
        part = q_all.at[x_far, r, pl.ds(128, 128)]
        remote(part, part, q_s.at[3, j], q_r.at[3, j], (xm, me)).wait_recv()
    for index, device in enumerate((x_down, x_up, x_far)):
        dst = used_all.at[device]
        remote(dst, dst, us_s.at[index], us_r.at[index], (xp, me)).wait_recv()
    for chunk in (5, 6):
        for direction in range(2):
            kv_land(direction, chunk)
    for copy in stores + out_copies:
        copy.wait()
    for copy in sends:
        copy.wait_send()


def attend_kernel(
    used_s, len_s, idx_s, q_all, k_all, v_all, new_k, new_v, anc, cache_k, cache_v,
    o_part, stats, acc_k, acc_v,
    qv, kv, vv, nkv, nvv, ancv, ckv, cvv, mb, accb, ob, stb, stt, sem, out_sem,
):
    batch, me, z, x, y, core = place()
    loads = [
        pltpu.make_async_copy(q_all, qv, sem.at[0]),
        pltpu.make_async_copy(k_all, kv, sem.at[1]),
        pltpu.make_async_copy(v_all, vv.at[:, :, pl.ds(0, HD)], sem.at[2]),
        pltpu.make_async_copy(new_k, nkv, sem.at[3]),
        pltpu.make_async_copy(new_v, nvv.at[:, :, pl.ds(0, HD)], sem.at[4]),
        pltpu.make_async_copy(anc, ancv, sem.at[5]),
        pltpu.make_async_copy(cache_k, ckv, sem.at[6]),
        pltpu.make_async_copy(cache_v, cvv.at[:, pl.ds(0, HD)], sem.at[7]),
    ]
    for load in loads:
        load.start()
    vv[:, :, HD:] = jnp.ones((NZ, BLOCK, HD), BF16)
    nvv[:, :, HD:] = jnp.ones((REQ, TREE, HD), BF16)
    cvv[:, HD:] = jnp.ones((cvv.shape[0], HD), BF16)
    for load in loads[:3]:
        load.wait()

    def absorb(query, keys, values, mask):
        scores = lax.dot_general(query, keys, (((1,), (1,)), ((), ())), preferred_element_type=F32)
        if mask is not None:
            scores = jnp.where(mask(scores.shape), scores, NEG_FILL)
        old = mb[...]
        new = jnp.maximum(old, jnp.max(scores, axis=1, keepdims=True))
        weights = jnp.exp2((scores - new[:, :1]) * SCALE2).astype(BF16)
        factor = jnp.exp2((old - new) * SCALE2)
        mb[...] = new
        accb[...] = accb[...] * jnp.concatenate([factor, factor], axis=1) + jnp.dot(
            weights, values, preferred_element_type=F32
        )

    lane = lax.broadcasted_iota(jnp.int32, (256, HD), 1)

    def one_request(i, _):
        group = lax.div(i, REQ)
        r = lax.rem(i, REQ)
        peer = lax.rem(x + 1 + group, NX)
        query = qv[peer, r]
        used = used_s[peer, 0, r] - BLOCK * x
        full = lax.min(lax.div(used - BLOCK, BLOCK * NX) + 1, NZ)
        mb[...] = jnp.full((256, HD), NEG_FILL, F32)
        accb[...] = jnp.zeros((256, 2 * HD), F32)

        def block(b, _):
            absorb(query, kv[b], vv[b], None)
            return 0

        lax.fori_loop(0, full, block, 0)
        rest = used - full * (BLOCK * NX)

        @pl.when(jnp.logical_and(rest > 0, full < NZ))
        def _():
            absorb(query, kv[full], vv[full], lambda s: lax.broadcasted_iota(jnp.int32, s, 1) < rest)

        @pl.when(i == REQ * (NX - 1))
        def _():
            for load in loads[3:]:
                load.wait()

        @pl.when(group == NX - 1)
        def _():
            lower = lax.fori_loop(0, r, lambda p, t: t + len_s[batch * REQ + p], 0)
            upper = lower + len_s[batch * REQ + r]
            first = lax.div(lower, 16) * 16
            count = lax.div(upper - first + CACHE_BLOCK - 1, CACHE_BLOCK)

            def cache_step(b, _):
                begin = first + b * CACHE_BLOCK
                start = pl.multiple_of(lax.min(begin, cache_k.shape[0] - CACHE_BLOCK), 16)
                rows = pl.ds(start, CACHE_BLOCK)

                def mask(s):
                    slot = start + lax.broadcasted_iota(jnp.int32, s, 1)
                    return (slot >= lax.max(lower, begin)) & (slot < upper)

                absorb(query, ckv[rows, :], cvv[rows, :], mask)
                return 0

            lax.fori_loop(0, count, cache_step, 0)
            table = ancv[pl.ds(pl.multiple_of(r * TREE, TREE), TREE), :] > 0.5

            def tree_mask(s):
                tall = ancv[pl.ds(pl.multiple_of(r * TREE, TREE), TREE), :]
                return jnp.concatenate([tall] * GROUP, axis=0) > 0.5

            absorb(query, nkv[r], nvv[r], tree_mask)

        total = accb[...]
        ob[peer, r] = (total[:, :HD] / total[:, HD:]).astype(BF16)
        level = mb[...] * SCALE2 + jnp.log2(total[:, HD:])
        stb[...] = jnp.where(lane == r, level, stb[...])

        @pl.when(r == REQ - 1)
        def _():
            stt[peer] = stb[...].T[:8, :]

        return 0

    stb[...] = jnp.zeros((256, HD), F32)
    lax.fori_loop(0, REQ * NX, one_request, 0)
    outs = [
        pltpu.make_async_copy(ob, o_part, out_sem.at[0]),
        pltpu.make_async_copy(stt, stats, out_sem.at[1]),
    ]
    for out in outs:
        out.start()
    row = lax.broadcasted_iota(jnp.int32, (8, TREE), 0)
    col = lax.broadcasted_iota(jnp.int32, (8, TREE), 1)
    for r in range(REQ):
        pick = jnp.zeros((8, TREE), F32)
        for p in range(8):
            pick = jnp.where((row == p) & (col == idx_s[r, p]), 1.0, pick)
        pick = pick.astype(BF16)
        acc_k[r] = jnp.dot(pick, nkv[r], preferred_element_type=F32).astype(BF16)
        acc_v[r] = jnp.dot(pick, nvv[r, :, pl.ds(0, HD)], preferred_element_type=F32).astype(BF16)
    for out in outs:
        out.wait()


def mix_kernel(
    o_part, stats, w_out,
    out,
    wv, own, got, ownst, gotst, relay, att, pb, pr, sb, far, yb, yr,
    s_s, s_r, x_s, x_r, p_s, p_r, f_s, f_r, y_s, y_r, loc,
):
    batch, me, z, x, y, core = place()
    yup, ydown, yfar = lax.rem(y + 1, NY), lax.rem(y + 3, NY), lax.rem(y + 2, NY)
    yp, ym, other = yup * 2 + core, ydown * 2 + core, y * 2 + 1 - core
    x_up, x_down, x_far = lax.rem(x + 1, NX), lax.rem(x + 3, NX), lax.rem(x + 2, NX)
    xp, xm, xf = z * NX + x_up, z * NX + x_down, z * NX + x_far
    loads = [
        pltpu.make_async_copy(w_out, wv, loc.at[0]),
        pltpu.make_async_copy(o_part.at[x], own, loc.at[1]),
        pltpu.make_async_copy(stats.at[x], ownst, loc.at[2]),
    ]
    for load in loads:
        load.start()
    greet([(batch, yp), (batch, ym), (batch, other), (xp, me), (xm, me), (xf, me)])
    sends = []

    def go(copy):
        copy.start()
        sends.append(copy)

    turn = (yfar, yup, ydown, y)
    first, second = pl.ds(0, 128), pl.ds(128, 128)
    peers = ((x_up, xp), (x_down, xm), (x_far, xf))
    for index, (peer, target) in enumerate(peers):
        go(remote(stats.at[peer], gotst.at[index], s_s.at[index], s_r.at[index], (target, me)))

    for j in range(REQ):
        r = turn[j]
        go(remote(o_part.at[x_far, r, first], relay.at[0, j], x_s.at[0, j], x_r.at[0, j], (xp, me)))
        go(remote(o_part.at[x_far, r, second], relay.at[1, j], x_s.at[1, j], x_r.at[1, j], (xm, me)))
        go(remote(o_part.at[x_up, r], got.at[0, r], x_s.at[2, j], x_r.at[2, j], (xp, me)))
        go(remote(o_part.at[x_down, r], got.at[1, r], x_s.at[3, j], x_r.at[3, j], (xm, me)))

    def pass_on(j):
        r = turn[j]
        for side, (rows, target) in enumerate(((first, xp), (second, xm))):
            slot = relay.at[side, j]
            remote(slot, slot, x_s.at[side, j], x_r.at[side, j], (target, me)).wait_recv()
            go(remote(slot, got.at[2, r, rows], x_s.at[4 + side, j], x_r.at[4 + side, j], (target, me)))

    for load in loads:
        load.wait()
    for index in range(3):
        slot = gotst.at[index]
        remote(slot, slot, s_s.at[index], s_r.at[index], (xp, me)).wait_recv()
    pass_on(0)
    levels = [ownst[...]] + [gotst[index] for index in range(3)]
    most = levels[0]
    for level in levels[1:]:
        most = jnp.maximum(most, level)
    powers = [jnp.exp2(level - most) for level in levels]
    whole = powers[0] + powers[1] + powers[2] + powers[3]
    shares = [(power / whole).T for power in powers]
    lane = lax.broadcasted_iota(jnp.int32, (256, 8), 1)

    def blend(j):
        r = turn[j]
        for kind in (2, 3):
            slot = got.at[kind - 2, r]
            remote(slot, slot, x_s.at[kind, j], x_r.at[kind, j], (xp, me)).wait_recv()
        for kind, rows in ((4, first), (5, second)):
            slot = got.at[2, r, rows]
            remote(slot, slot, x_s.at[kind, j], x_r.at[kind, j], (xp, me)).wait_recv()
        total = jnp.zeros((256, HD), F32)
        for index in range(4):
            piece = own[r] if index == 0 else got[index - 1, r]
            share = jnp.sum(jnp.where(lane == r, shares[index], 0.0), axis=1, keepdims=True)
            total = total + share * piece.astype(F32)
        total = total.astype(BF16)
        for g in range(GROUP):
            att[:, pl.ds(g * HD, HD)] = total[g * TREE : (g + 1) * TREE, :]

        def columns(n, _):
            cols = pl.ds(pl.multiple_of(n * 1024, 1024), 1024)
            part = jnp.dot(att[...], wv[:, cols], preferred_element_type=F32).astype(BF16)
            pb[j, 0, :, cols] = part[:32, :]
            pb[j, 1, :, cols] = part[32:, :]
            return 0

        lax.fori_loop(0, 4, columns, 0)
        go(remote(pb.at[j, 1 - core], pr.at[j], p_s.at[j], p_r.at[j], (batch, other)))

    def pair_sum(j):
        slot = pr.at[j]
        remote(slot, slot, p_s.at[j], p_r.at[j], (batch, other)).wait_recv()
        return pb[j, core].astype(F32) + pr[j].astype(F32)

    top, low = pl.ds(0, 16), pl.ds(16, 16)
    blend(0)
    pass_on(1)
    blend(1)
    sb[...] = pair_sum(0).astype(BF16)
    go(remote(sb.at[top], far.at[0], f_s.at[0], f_r.at[0], (batch, yp)))
    go(remote(sb.at[low], far.at[1], f_s.at[1], f_r.at[1], (batch, ym)))
    pass_on(2)
    blend(2)
    slot = far.at[0]
    remote(slot, slot, f_s.at[0], f_r.at[0], (batch, yp)).wait_recv()
    value = pair_sum(1)
    yb[0, top, :] = (value[:16, :] + far[0].astype(F32)).astype(BF16)
    yb[0, low, :] = value[16:, :].astype(BF16)
    go(remote(yb.at[0], yr.at[0], y_s.at[0], y_r.at[0], (batch, yp)))
    pass_on(3)
    slot = far.at[1]
    remote(slot, slot, f_s.at[1], f_r.at[1], (batch, ym)).wait_recv()
    value = pair_sum(2)
    yb[1, top, :] = value[:16, :].astype(BF16)
    yb[1, low, :] = (value[16:, :] + far[1].astype(F32)).astype(BF16)
    go(remote(yb.at[1], yr.at[1], y_s.at[1], y_r.at[1], (batch, ym)))
    blend(3)
    value = pair_sum(3)
    for index in range(2):
        slot = yr.at[index]
        remote(slot, slot, y_s.at[index], y_r.at[index], (batch, yp)).wait_recv()
        value = value + yr[index].astype(F32)
    out[...] = value.astype(BF16)
    for copy in sends:
        copy.wait_send()


def body(
    tokens, norm_gain, w_query, w_key, w_value, w_out, prefix_keys, prefix_values,
    cache_keys, cache_values, cache_lengths, prefix_used, parents, accepted_index,
):
    exponents = -jnp.arange(HD // 2, dtype=F32) / (HD // 2)
    frequency = jnp.tile(10000.0 ** exponents, 2)[None, :]
    any_spec = pl.BlockSpec(memory_space=pl.ANY)
    smem = pl.BlockSpec(memory_space=pltpu.SMEM)
    vmem = pl.BlockSpec(memory_space=pltpu.VMEM)
    dma = pltpu.SemaphoreType.DMA
    shape = jax.ShapeDtypeStruct
    limit = 60 * 1024 * 1024
    q_all, k_all, v_all, new_k, new_v, anc, used_all = pl.pallas_call(
        project_kernel,
        out_shape=(
            shape((NX, REQ, 256, HD), BF16),
            shape((NZ, BLOCK, HD), BF16),
            shape((NZ, BLOCK, HD), BF16),
            shape((REQ, TREE, HD), BF16),
            shape((REQ, TREE, HD), BF16),
            shape((REQ * TREE, TREE), F32),
            shape((NX, 8, HD), jnp.int32),
        ),
        in_specs=[smem, smem, vmem, vmem, vmem] + [any_spec] * 6,
        out_specs=[any_spec] * 7,
        scratch_shapes=[
            pltpu.VMEM((8, 32, 4096), BF16),
            pltpu.VMEM((4096, 768), BF16),
            pltpu.VMEM((TREE, 4096), BF16),
            pltpu.VMEM((REQ, 256, HD), BF16),
            pltpu.VMEM((REQ, TREE, HD), BF16),
            pltpu.VMEM((REQ, TREE, HD), BF16),
            pltpu.VMEM((REQ * TREE, TREE), F32),
            pltpu.VMEM((8, HD), jnp.int32),
            pltpu.VMEM((REQ, TREE, HD), F32),
            pltpu.VMEM((REQ, TREE, HD), F32),
            pltpu.VMEM((2, BLOCK, HD), BF16),
            dma((11,)), dma((11,)), dma((2, 7)), dma((2, 7)), dma((4, REQ)), dma((4, REQ)), dma((3,)), dma((3,)),
            dma((8,)),
        ],
        compiler_params=pltpu.CompilerParams(collective_id=0, has_side_effects=True, vmem_limit_bytes=limit),
        name="project_and_gather",
    )(
        prefix_used, cache_lengths, parents, norm_gain[None, :], frequency, tokens, w_query, w_key, w_value,
        prefix_keys, prefix_values,
    )
    slots = cache_keys.shape[0]
    o_part, stats, acc_k, acc_v = pl.pallas_call(
        attend_kernel,
        out_shape=(
            shape((NX, REQ, 256, HD), BF16),
            shape((NX, 8, 256), F32),
            shape((REQ, 8, HD), BF16),
            shape((REQ, 8, HD), BF16),
        ),
        in_specs=[smem, smem, smem] + [any_spec] * 8,
        out_specs=[any_spec, any_spec, vmem, vmem],
        scratch_shapes=[
            pltpu.VMEM((NX, REQ, 256, HD), BF16),
            pltpu.VMEM((NZ, BLOCK, HD), BF16),
            pltpu.VMEM((NZ, BLOCK, 2 * HD), BF16),
            pltpu.VMEM((REQ, TREE, HD), BF16),
            pltpu.VMEM((REQ, TREE, 2 * HD), BF16),
            pltpu.VMEM((REQ * TREE, TREE), F32),
            pltpu.VMEM((slots, HD), BF16),
            pltpu.VMEM((slots, 2 * HD), BF16),
            pltpu.VMEM((256, HD), F32),
            pltpu.VMEM((256, 2 * HD), F32),
            pltpu.VMEM((NX, REQ, 256, HD), BF16),
            pltpu.VMEM((256, HD), F32),
            pltpu.VMEM((NX, 8, 256), F32),
            dma((8,)), dma((2,)),
        ],
        compiler_params=pltpu.CompilerParams(vmem_limit_bytes=limit),
        name="attend",
    )(
        used_all, cache_lengths, accepted_index, q_all, k_all, v_all, new_k, new_v, anc, cache_keys, cache_values
    )
    mixed = pl.pallas_call(
        mix_kernel,
        out_shape=shape((32, 4096), BF16),
        in_specs=[any_spec] * 3,
        out_specs=vmem,
        scratch_shapes=[
            pltpu.VMEM((512, 4096), BF16),
            pltpu.VMEM((REQ, 256, HD), BF16),
            pltpu.VMEM((3, REQ, 256, HD), BF16),
            pltpu.VMEM((8, 256), F32),
            pltpu.VMEM((3, 8, 256), F32),
            pltpu.VMEM((2, REQ, 128, HD), BF16),
            pltpu.VMEM((TREE, 512), BF16),
            pltpu.VMEM((REQ, 2, 32, 4096), BF16),
            pltpu.VMEM((REQ, 32, 4096), BF16),
            pltpu.VMEM((32, 4096), BF16),
            pltpu.VMEM((2, 16, 4096), BF16),
            pltpu.VMEM((2, 32, 4096), BF16),
            pltpu.VMEM((2, 32, 4096), BF16),
            dma((3,)), dma((3,)), dma((6, REQ)), dma((6, REQ)), dma((REQ,)), dma((REQ,)), dma((2,)), dma((2,)),
            dma((2,)), dma((2,)), dma((3,)),
        ],
        compiler_params=pltpu.CompilerParams(collective_id=1, has_side_effects=True, vmem_limit_bytes=limit),
        name="mix",
    )(o_part, stats, w_out)
    return (mixed, acc_k, acc_v)


def solution(mesh):
    in_specs = (
        P(("batch", "tensor"), None),
        P(),
        P(None, "tensor"),
        P(None, "tensor"),
        P(None, "tensor"),
        P("tensor", None),
        P("batch", "tensor"),
        P("batch", "tensor"),
        P("batch", "tensor"),
        P("batch", "tensor"),
        P(),
        P("batch"),
        P("batch", None),
        P("batch", None),
    )
    out_specs = (
        P(("batch", "tensor"), None),
        P("batch", None, "tensor"),
        P("batch", None, "tensor"),
    )
    return jax.shard_map(body, mesh=mesh, in_specs=in_specs, out_specs=out_specs, check_vma=False)
```

```python
import jax
import jax.numpy as jnp
from jax import lax
from jax.experimental import pallas as pl
from jax.experimental.pallas import tpu as pltpu
from jax.sharding import PartitionSpec as P

HD = 128
TREE = 64
GROUP = 4
REQ = 4
NX = 4
NZ = 8
NY = 4
BLOCK = 512
ITEMS = REQ * NX + REQ
NEG_FILL = -1e30
LOG2E = 1.4426950408889634
SCALE2 = HD ** (-0.5) * LOG2E
MESH = pl.DeviceIdType.MESH
ORDER = (0, 1, 3, 2)
F32 = jnp.float32
BF16 = jnp.bfloat16


def place():
    batch = lax.axis_index("batch")
    tensor = lax.axis_index("tensor")
    z, x = lax.div(batch, NX), lax.rem(batch, NX)
    y, core = lax.div(tensor, 2), lax.rem(tensor, 2)
    return batch, tensor, z, x, y, core


def remote(src, dst, send, recv, device):
    return pltpu.make_async_remote_copy(
        src_ref=src, dst_ref=dst, send_sem=send, recv_sem=recv, device_id=device, device_id_type=MESH
    )


def greet(devices):
    barrier = pltpu.get_barrier_semaphore()
    for device in devices:
        pl.semaphore_signal(barrier, inc=1, device_id=device, device_id_type=MESH)
    pl.semaphore_wait(barrier, len(devices))


def project_kernel(
    used_s, len_s, par, gain, freq, tok, wq, wk, wv, pk, pv,
    q_all, k_all, v_all, new_k, new_v, anc, used_all,
    tokb, wb, normb, qb, nkb, nvb, ancb, usedb, cosb, sinb, kvb,
    tok_s, tok_r, kv_s, kv_r, q_s, q_r, us_s, us_r, loc,
):
    batch, me, z, x, y, core = place()
    yp = lax.rem(y + 1, NY) * 2 + core
    ym = lax.rem(y + 3, NY) * 2 + core
    y2 = lax.rem(y + 2, NY) * 2 + core
    other = y * 2 + 1 - core
    oyp = lax.rem(y + 1, NY) * 2 + 1 - core
    oym = lax.rem(y + 3, NY) * 2 + 1 - core
    oy2 = lax.rem(y + 2, NY) * 2 + 1 - core
    zp = lax.rem(z + 1, NZ) * NX + x
    zm = lax.rem(z + NZ - 1, NZ) * NX + x
    x_up, x_down, x_far = lax.rem(x + 1, NX), lax.rem(x + 3, NX), lax.rem(x + 2, NX)
    xp, xm, xf = z * NX + x_up, z * NX + x_down, z * NX + x_far
    top, low = pl.ds(0, 16), pl.ds(16, 16)

    loads = [
        pltpu.make_async_copy(tok, tokb.at[me], loc.at[0]),
        pltpu.make_async_copy(wq, wb.at[:, pl.ds(0, 512)], loc.at[1]),
        pltpu.make_async_copy(wk, wb.at[:, pl.ds(512, 128)], loc.at[2]),
        pltpu.make_async_copy(wv, wb.at[:, pl.ds(640, 128)], loc.at[3]),
        pltpu.make_async_copy(pk, kvb.at[0], loc.at[4]),
        pltpu.make_async_copy(pv, kvb.at[1], loc.at[5]),
    ]
    for load in loads:
        load.start()

    lane = lax.broadcasted_iota(jnp.int32, (8, HD), 1)
    used_row = jnp.zeros((8, HD), jnp.int32)
    for r in range(REQ):
        used_row = jnp.where(lane == r, used_s[r], used_row)
    usedb[...] = used_row

    greet([(batch, yp), (batch, ym), (batch, other), (zp, me), (zm, me), (xp, me), (xm, me), (xf, me)])

    def tok_copy(index, src, slot, rows, target):
        dst = tokb.at[slot] if rows is None else tokb.at[slot, rows]
        return remote(src, dst, tok_s.at[index], tok_r.at[index], (batch, target))

    def tok_land(index, slot, rows):
        dst = tokb.at[slot] if rows is None else tokb.at[slot, rows]
        return remote(dst, dst, tok_s.at[index], tok_r.at[index], (batch, other))

    sends = []

    def go(copy):
        copy.start()
        sends.append(copy)

    def kv_parts(direction, chunk):
        hop = chunk // 2
        is_key = (chunk + direction) % 2 == 0
        gathered = k_all if is_key else v_all
        own = pk if is_key else pv
        return hop, gathered, own

    def kv_send(direction, chunk):
        hop, gathered, own = kv_parts(direction, chunk)
        if direction == 0:
            block, target = lax.rem(z + NZ - hop, NZ), zp
        else:
            block, target = lax.rem(z + hop, NZ), zm
        src = own if hop == 0 else gathered.at[block]
        go(remote(src, gathered.at[block], kv_s.at[direction, chunk], kv_r.at[direction, chunk], (target, me)))

    def kv_land(direction, chunk):
        hop, gathered, own = kv_parts(direction, chunk)
        if direction == 0:
            block = lax.rem(z + NZ - 1 - hop, NZ)
        else:
            block = lax.rem(z + 1 + hop, NZ)
        dst = gathered.at[block]
        remote(dst, dst, kv_s.at[direction, chunk], kv_r.at[direction, chunk], (zp, me)).wait_recv()

    def kv_step(chunk):
        for direction in range(2):
            kv_land(direction, chunk - 2)
            kv_send(direction, chunk)

    go(tok_copy(0, tok.at[top], me, top, yp))
    go(tok_copy(2, tok.at[low], me, low, ym))
    for direction in range(2):
        kv_send(direction, 0)
    go(tok_copy(4, tok, me, None, other))
    go(tok_copy(1, tok.at[low], me, low, yp))
    go(tok_copy(3, tok.at[top], me, top, ym))
    for direction in range(2):
        kv_send(direction, 1)
    for index, (target, device) in enumerate(((xp, x_up), (xm, x_down), (xf, x_far))):
        go(remote(usedb, used_all.at[x], us_s.at[index], us_r.at[index], (target, me)))

    row = lax.broadcasted_iota(jnp.int32, (TREE, TREE), 0)
    col = lax.broadcasted_iota(jnp.int32, (TREE, TREE), 1)
    tables = []
    for r in range(REQ):
        hit = (row == par[pl.ds(r, 1), :]) | (row == col)
        tables.append(jnp.where(hit, 1.0, 0.0))
    for repeat in range(6):
        tables = [
            jnp.minimum(jnp.dot(a.astype(BF16), a.astype(BF16), preferred_element_type=F32), 1.0) for a in tables
        ]
    upper = lax.broadcasted_iota(jnp.int32, (TREE, HD), 1) < HD // 2
    for r in range(REQ):
        table = tables[r].T
        ancb[r] = jnp.concatenate([tables[r]] * GROUP, axis=1)
        depth = jnp.sum(table, axis=1, keepdims=True) - 1.0
        base = (used_s[r] + len_s[batch * REQ + r]).astype(F32)
        angles = (depth + base) * freq[...]
        cosb[r] = jnp.cos(angles)
        sine = jnp.sin(angles)
        sinb[r] = jnp.where(upper, -sine, sine)

    for load in loads:
        load.wait()
    stores = [
        pltpu.make_async_copy(kvb.at[0], k_all.at[z], loc.at[4]),
        pltpu.make_async_copy(kvb.at[1], v_all.at[z], loc.at[5]),
        pltpu.make_async_copy(usedb, used_all.at[x], loc.at[6]),
        pltpu.make_async_copy(ancb, anc, loc.at[7]),
    ]
    for store in stores:
        store.start()

    def request_of(j):
        return lax.rem(y + ORDER[j], NY)

    def project(j):
        r = request_of(j)
        for half in range(2):
            values = tokb[2 * r + half].astype(F32)
            factor = lax.rsqrt(jnp.mean(values * values, axis=-1, keepdims=True) + 1e-05)
            normb[pl.ds(half * 32, 32), :] = (values * factor * gain[...]).astype(BF16)

        def step(k, total):
            rows = pl.ds(pl.multiple_of(k * 512, 512), 512)
            return total + jnp.dot(normb[:, rows], wb[rows, :], preferred_element_type=F32)

        total = lax.fori_loop(0, 8, step, jnp.zeros((TREE, 768), F32))
        cosine, sine = cosb[r], sinb[r]

        def turn(head):
            return (head * cosine + pltpu.roll(head, HD // 2, 1) * sine).astype(BF16)

        for g in range(GROUP):
            qb[r, pl.ds(g * TREE, TREE), :] = turn(total[:, g * HD : (g + 1) * HD])
        nkb[r] = turn(total[:, 512:640])
        nvb[r] = total[:, 640:768].astype(BF16)
        go(remote(qb.at[r], q_all.at[x, r], q_s.at[0, j], q_r.at[0, j], (xp, me)))
        go(remote(qb.at[r], q_all.at[x, r], q_s.at[1, j], q_r.at[1, j], (xm, me)))

    def q_relay(j):
        r = request_of(j)
        lower = q_all.at[x_down, r]
        remote(lower, lower, q_s.at[0, j], q_r.at[0, j], (xp, me)).wait_recv()
        part = q_all.at[x_down, r, pl.ds(0, 128)]
        go(remote(part, part, q_s.at[2, j], q_r.at[2, j], (xp, me)))
        higher = q_all.at[x_up, r]
        remote(higher, higher, q_s.at[1, j], q_r.at[1, j], (xm, me)).wait_recv()
        part = q_all.at[x_up, r, pl.ds(128, 128)]
        go(remote(part, part, q_s.at[3, j], q_r.at[3, j], (xm, me)))

    tok_land(0, ym, top).wait_recv()
    go(tok_copy(5, tokb.at[ym, top], ym, top, yp))
    tok_land(2, yp, low).wait_recv()
    go(tok_copy(6, tokb.at[yp, low], yp, low, ym))
    kv_step(2)
    tok_land(4, other, None).wait_recv()
    project(0)
    tok_land(3, yp, top).wait_recv()
    go(tok_copy(8, tokb.at[yp], yp, None, other))
    tok_land(1, ym, low).wait_recv()
    go(tok_copy(7, tokb.at[ym], ym, None, other))
    kv_step(3)
    tok_land(8, oyp, None).wait_recv()
    project(1)
    q_relay(0)
    tok_land(5, y2, top).wait_recv()
    go(tok_copy(9, tokb.at[y2, top], y2, top, other))
    tok_land(6, y2, low).wait_recv()
    go(tok_copy(10, tokb.at[y2, low], y2, low, other))
    kv_step(4)
    tok_land(7, oym, None).wait_recv()
    project(2)
    q_relay(1)
    kv_step(5)
    tok_land(9, oy2, top).wait_recv()
    tok_land(10, oy2, low).wait_recv()
    project(3)
    out_copies = [
        pltpu.make_async_copy(qb, q_all.at[x], loc.at[0]),
        pltpu.make_async_copy(nkb, new_k, loc.at[1]),
        pltpu.make_async_copy(nvb, new_v, loc.at[2]),
    ]
    for copy in out_copies:
        copy.start()
    kv_step(6)
    q_relay(2)
    q_relay(3)
    for j in range(REQ):
        r = request_of(j)
        part = q_all.at[x_far, r, pl.ds(0, 128)]
        remote(part, part, q_s.at[2, j], q_r.at[2, j], (xp, me)).wait_recv()
        part = q_all.at[x_far, r, pl.ds(128, 128)]
        remote(part, part, q_s.at[3, j], q_r.at[3, j], (xm, me)).wait_recv()
    for index, device in enumerate((x_down, x_up, x_far)):
        dst = used_all.at[device]
        remote(dst, dst, us_s.at[index], us_r.at[index], (xp, me)).wait_recv()
    for chunk in (5, 6):
        for direction in range(2):
            kv_land(direction, chunk)
    for copy in stores + out_copies:
        copy.wait()
    for copy in sends:
        copy.wait_send()


def attend_kernel(
    used_s, len_s, idx_s, q_all, k_all, v_all, new_k, new_v, anc, cache_k, cache_v,
    o_part, stats, acc_k, acc_v,
    qv, kv, vb, vt, nkv, nvv, ancv, sc, mb, accb, ob, lv, stt, items, order, sem, out_sem,
):
    batch, me, z, x, y, core = place()
    prefix_rows = NZ * BLOCK
    slots = cache_k.shape[0]
    loads = [
        pltpu.make_async_copy(v_all, vb.at[pl.ds(0, prefix_rows)], sem.at[0]),
        pltpu.make_async_copy(cache_v, vb.at[pl.ds(prefix_rows, slots)], sem.at[1]),
        pltpu.make_async_copy(k_all, kv.at[pl.ds(0, prefix_rows)], sem.at[2]),
        pltpu.make_async_copy(cache_k, kv.at[pl.ds(prefix_rows, slots)], sem.at[3]),
        pltpu.make_async_copy(q_all, qv, sem.at[4]),
        pltpu.make_async_copy(new_k, nkv, sem.at[5]),
        pltpu.make_async_copy(new_v, nvv, sem.at[6]),
        pltpu.make_async_copy(anc, ancv, sem.at[7]),
    ]
    for load in loads:
        load.start()

    def note(i, blocks, query, first, lower, upper):
        for field, value in enumerate((blocks, query, first, lower, upper)):
            items[field, i] = value

    def prefix_item(i, _):
        used = used_s[lax.div(i, REQ), 0, lax.rem(i, REQ)] - BLOCK * x
        full = lax.min(lax.div(used - BLOCK, BLOCK * NX) + 1, NZ)
        rest = jnp.where(full < NZ, lax.max(used - full * (BLOCK * NX), 0), 0)
        note(i, full + jnp.where(rest > 0, 1, 0), i, 0, 0, full * BLOCK + rest)
        return 0

    def cache_item(r, lower):
        upper = lower + len_s[batch * REQ + r]
        first = lax.div(lower, 128) * 128
        blocks = lax.div(upper - first + BLOCK - 1, BLOCK)
        first = lax.min(first, slots - blocks * BLOCK)
        note(REQ * NX + r, blocks, x * REQ + r, prefix_rows + first, lower - first, upper - first)
        return upper

    lax.fori_loop(0, REQ * NX, prefix_item, 0)
    lax.fori_loop(0, REQ, cache_item, 0)

    def by_size(v, spot):
        def put(i, spot):
            order[spot] = i
            return spot + jnp.where(items[0, i] == NZ - v, 1, 0)

        return lax.fori_loop(0, ITEMS, put, spot)

    lax.fori_loop(0, NZ, by_size, 0)

    vt[HD:, :] = jnp.ones((16, vt.shape[1]), BF16)
    loads[0].wait()
    for n in range(NZ):
        vt[:HD, n * BLOCK : (n + 1) * BLOCK] = vb[n * BLOCK : (n + 1) * BLOCK, :].T
    loads[1].wait()
    for n in range(NZ, (prefix_rows + slots) // BLOCK):
        vt[:HD, n * BLOCK : (n + 1) * BLOCK] = vb[n * BLOCK : (n + 1) * BLOCK, :].T
    for load in loads[2:]:
        load.wait()

    def dot_last(a, b):
        return lax.dot_general(a, b, (((1,), (1,)), ((), ())), preferred_element_type=F32)

    def fold(values, op):
        while values.shape[0] > 8:
            half = values.shape[0] // 2
            values = op(values[:half], values[half:])
        return values

    row = lax.broadcasted_iota(jnp.int32, (BLOCK, HD), 0)

    def score(item, slot, b):
        rows = pl.ds(pl.multiple_of(items[2, item] + b * BLOCK, 128), BLOCK)
        values = dot_last(kv[rows, :], qv[items[1, item]])
        place_row = row + b * BLOCK
        seen = (place_row >= items[3, item]) & (place_row < items[4, item])
        for side in range(2):
            lanes = slice(side * HD, (side + 1) * HD)
            part = jnp.where(seen, values[:, lanes], NEG_FILL)
            sc[slot, pl.ds(b * BLOCK, BLOCK), lanes] = part
            best = part[:64]
            for j in range(1, BLOCK // 64):
                best = jnp.maximum(best, part[j * 64 : (j + 1) * 64])
            mb[slot, :, lanes] = jnp.maximum(mb[slot, :, lanes], fold(best, jnp.maximum))

    def gather_values(item, slot, b):
        cols = pl.ds(pl.multiple_of(items[2, item] + b * BLOCK, 128), BLOCK)
        weights = jnp.exp2((sc[slot, pl.ds(b * BLOCK, BLOCK), :] - mb[slot, :1, :]) * SCALE2).astype(BF16)
        return jnp.dot(vt[:, cols], weights, preferred_element_type=F32)

    def clear(slot):
        mb[slot] = jnp.full((8, 256), NEG_FILL, F32)

    clear(0)
    lead = order[0]
    for b in range(NZ):

        @pl.when(b < items[0, lead])
        def _():
            score(lead, 0, b)

    def pair(h, _):
        for slot in range(2):
            item = order[2 * h + slot]
            after = order[lax.min(2 * h + slot + 1, ITEMS - 1)]
            mb[slot] = jnp.broadcast_to(jnp.max(mb[slot], axis=0, keepdims=True), (8, 256))
            clear(1 - slot)
            for size in range(1, NZ + 1):

                @pl.when(items[0, item] == size)
                def _():
                    total = None
                    for b in range(size):
                        part = gather_values(item, slot, b)
                        total = part if total is None else total + part
                        score(after, 1 - slot, b)
                    accb[...] = total

            mass = accb[HD : HD + 1, :]
            ob[item] = (accb[:HD, :] / mass).astype(BF16)
            lv[item] = jnp.broadcast_to(mb[slot, :1, :] * SCALE2 + jnp.log2(mass), (8, 256))
        return 0

    lax.fori_loop(0, ITEMS // 2, pair, 0)

    for r in range(REQ):
        values = dot_last(nkv[r], qv[x * REQ + r])
        values = jnp.where(ancv[r] > 0.5, values, NEG_FILL)
        best = jnp.max(values, axis=0, keepdims=True)
        weights = jnp.exp2((values - best) * SCALE2)
        mass = jnp.sum(weights, axis=0, keepdims=True)
        tree_out = jnp.dot(nvv[r].T, weights.astype(BF16), preferred_element_type=F32) / mass
        levels = (best * SCALE2 + jnp.log2(mass), lv[x * REQ + r, :1, :], lv[REQ * NX + r, :1, :])
        top = jnp.maximum(jnp.maximum(levels[0], levels[1]), levels[2])
        shares = [jnp.exp2(level - top) for level in levels]
        whole = shares[0] + shares[1] + shares[2]
        merged = (
            shares[0] * tree_out
            + shares[1] * ob[x * REQ + r].astype(F32)
            + shares[2] * ob[REQ * NX + r].astype(F32)
        ) / whole
        ob[x * REQ + r] = merged.astype(BF16)
        lv[x * REQ + r] = jnp.broadcast_to(top + jnp.log2(whole), (8, 256))
    for peer in range(NX):
        for r in range(REQ):
            stt[peer, r : r + 1, :] = lv[peer * REQ + r, :1, :]
            stt[peer, REQ + r : REQ + r + 1, :] = lv[peer * REQ + r, :1, :]
    outs = [
        pltpu.make_async_copy(ob.at[pl.ds(0, REQ * NX)], o_part, out_sem.at[0]),
        pltpu.make_async_copy(stt, stats, out_sem.at[1]),
    ]
    for out in outs:
        out.start()
    row8 = lax.broadcasted_iota(jnp.int32, (8, TREE), 0)
    col8 = lax.broadcasted_iota(jnp.int32, (8, TREE), 1)
    for r in range(REQ):
        pick = jnp.zeros((8, TREE), F32)
        for p in range(8):
            pick = jnp.where((row8 == p) & (col8 == idx_s[r, p]), 1.0, pick)
        pick = pick.astype(BF16)
        acc_k[r] = jnp.dot(pick, nkv[r], preferred_element_type=F32).astype(BF16)
        acc_v[r] = jnp.dot(pick, nvv[r], preferred_element_type=F32).astype(BF16)
    for out in outs:
        out.wait()


def mix_kernel(
    o_part, stats, w_out,
    out,
    wv, own, got, ownst, gotst, shareb, relay, att, pb, pr, sb, far, yb, yr,
    s_s, s_r, x_s, x_r, p_s, p_r, f_s, f_r, y_s, y_r, loc,
):
    batch, me, z, x, y, core = place()
    yup, ydown, yfar = lax.rem(y + 1, NY), lax.rem(y + 3, NY), lax.rem(y + 2, NY)
    yp, ym, other = yup * 2 + core, ydown * 2 + core, y * 2 + 1 - core
    x_up, x_down, x_far = lax.rem(x + 1, NX), lax.rem(x + 3, NX), lax.rem(x + 2, NX)
    xp, xm, xf = z * NX + x_up, z * NX + x_down, z * NX + x_far
    loads = [
        pltpu.make_async_copy(w_out, wv, loc.at[0]),
        pltpu.make_async_copy(o_part.at[x], own, loc.at[1]),
        pltpu.make_async_copy(stats.at[x], ownst, loc.at[2]),
    ]
    for load in loads:
        load.start()
    greet([(batch, yp), (batch, ym), (batch, other), (xp, me), (xm, me), (xf, me)])
    sends = []

    def go(copy):
        copy.start()
        sends.append(copy)

    turn = (yfar, yup, ydown, y)
    first, second = pl.ds(0, 64), pl.ds(64, 64)
    peers = ((x_up, xp), (x_down, xm), (x_far, xf))
    for index, (peer, target) in enumerate(peers):
        go(remote(stats.at[peer], gotst.at[index], s_s.at[index], s_r.at[index], (target, me)))

    for j in range(REQ):
        r = turn[j]
        go(remote(o_part.at[x_far, r, first], relay.at[0, j], x_s.at[0, j], x_r.at[0, j], (xp, me)))
        go(remote(o_part.at[x_far, r, second], relay.at[1, j], x_s.at[1, j], x_r.at[1, j], (xm, me)))
        go(remote(o_part.at[x_up, r], got.at[0, r], x_s.at[2, j], x_r.at[2, j], (xp, me)))
        go(remote(o_part.at[x_down, r], got.at[1, r], x_s.at[3, j], x_r.at[3, j], (xm, me)))

    def pass_on(j):
        r = turn[j]
        for side, (rows, target) in enumerate(((first, xp), (second, xm))):
            slot = relay.at[side, j]
            remote(slot, slot, x_s.at[side, j], x_r.at[side, j], (target, me)).wait_recv()
            go(remote(slot, got.at[2, r, rows], x_s.at[4 + side, j], x_r.at[4 + side, j], (target, me)))

    for load in loads:
        load.wait()
    for index in range(3):
        slot = gotst.at[index]
        remote(slot, slot, s_s.at[index], s_r.at[index], (xp, me)).wait_recv()
    pass_on(0)
    levels = [ownst[...]] + [gotst[index] for index in range(3)]
    most = levels[0]
    for level in levels[1:]:
        most = jnp.maximum(most, level)
    powers = [jnp.exp2(level - most) for level in levels]
    whole = powers[0] + powers[1] + powers[2] + powers[3]
    for index in range(4):
        shareb[index] = powers[index] / whole

    def blend(j):
        r = turn[j]
        for kind in (2, 3):
            slot = got.at[kind - 2, r]
            remote(slot, slot, x_s.at[kind, j], x_r.at[kind, j], (xp, me)).wait_recv()
        for kind, rows in ((4, first), (5, second)):
            slot = got.at[2, r, rows]
            remote(slot, slot, x_s.at[kind, j], x_r.at[kind, j], (xp, me)).wait_recv()
        total = jnp.zeros((HD, 256), F32)
        for index in range(4):
            piece = own[r] if index == 0 else got[index - 1, r]
            total = total + shareb[index, pl.ds(r, 1), :] * piece.astype(F32)
        total = total.T.astype(BF16)
        for g in range(GROUP):
            att[:, pl.ds(g * HD, HD)] = total[g * TREE : (g + 1) * TREE, :]

        def columns(n, _):
            cols = pl.ds(pl.multiple_of(n * 1024, 1024), 1024)
            part = jnp.dot(att[...], wv[:, cols], preferred_element_type=F32).astype(BF16)
            pb[j, 0, :, cols] = part[:32, :]
            pb[j, 1, :, cols] = part[32:, :]
            return 0

        lax.fori_loop(0, 4, columns, 0)
        go(remote(pb.at[j, 1 - core], pr.at[j], p_s.at[j], p_r.at[j], (batch, other)))

    def pair_sum(j):
        slot = pr.at[j]
        remote(slot, slot, p_s.at[j], p_r.at[j], (batch, other)).wait_recv()
        return pb[j, core].astype(F32) + pr[j].astype(F32)

    top, low = pl.ds(0, 16), pl.ds(16, 16)
    blend(0)
    pass_on(1)
    blend(1)
    sb[...] = pair_sum(0).astype(BF16)
    go(remote(sb.at[top], far.at[0], f_s.at[0], f_r.at[0], (batch, yp)))
    go(remote(sb.at[low], far.at[1], f_s.at[1], f_r.at[1], (batch, ym)))
    pass_on(2)
    blend(2)
    slot = far.at[0]
    remote(slot, slot, f_s.at[0], f_r.at[0], (batch, yp)).wait_recv()
    value = pair_sum(1)
    yb[0, top, :] = (value[:16, :] + far[0].astype(F32)).astype(BF16)
    yb[0, low, :] = value[16:, :].astype(BF16)
    go(remote(yb.at[0], yr.at[0], y_s.at[0], y_r.at[0], (batch, yp)))
    pass_on(3)
    slot = far.at[1]
    remote(slot, slot, f_s.at[1], f_r.at[1], (batch, ym)).wait_recv()
    value = pair_sum(2)
    yb[1, top, :] = value[:16, :].astype(BF16)
    yb[1, low, :] = (value[16:, :] + far[1].astype(F32)).astype(BF16)
    go(remote(yb.at[1], yr.at[1], y_s.at[1], y_r.at[1], (batch, ym)))
    blend(3)
    value = pair_sum(3)
    for index in range(2):
        slot = yr.at[index]
        remote(slot, slot, y_s.at[index], y_r.at[index], (batch, yp)).wait_recv()
        value = value + yr[index].astype(F32)
    out[...] = value.astype(BF16)
    for copy in sends:
        copy.wait_send()


def body(
    tokens, norm_gain, w_query, w_key, w_value, w_out, prefix_keys, prefix_values,
    cache_keys, cache_values, cache_lengths, prefix_used, parents, accepted_index,
):
    exponents = -jnp.arange(HD // 2, dtype=F32) / (HD // 2)
    frequency = jnp.tile(10000.0 ** exponents, 2)[None, :]
    any_spec = pl.BlockSpec(memory_space=pl.ANY)
    smem = pl.BlockSpec(memory_space=pltpu.SMEM)
    vmem = pl.BlockSpec(memory_space=pltpu.VMEM)
    dma = pltpu.SemaphoreType.DMA
    shape = jax.ShapeDtypeStruct
    limit = 60 * 1024 * 1024
    q_all, k_all, v_all, new_k, new_v, anc, used_all = pl.pallas_call(
        project_kernel,
        out_shape=(
            shape((NX, REQ, 256, HD), BF16),
            shape((NZ, BLOCK, HD), BF16),
            shape((NZ, BLOCK, HD), BF16),
            shape((REQ, TREE, HD), BF16),
            shape((REQ, TREE, HD), BF16),
            shape((REQ, TREE, 256), F32),
            shape((NX, 8, HD), jnp.int32),
        ),
        in_specs=[smem, smem, vmem, vmem, vmem] + [any_spec] * 6,
        out_specs=[any_spec] * 7,
        scratch_shapes=[
            pltpu.VMEM((8, 32, 4096), BF16),
            pltpu.VMEM((4096, 768), BF16),
            pltpu.VMEM((TREE, 4096), BF16),
            pltpu.VMEM((REQ, 256, HD), BF16),
            pltpu.VMEM((REQ, TREE, HD), BF16),
            pltpu.VMEM((REQ, TREE, HD), BF16),
            pltpu.VMEM((REQ, TREE, 256), F32),
            pltpu.VMEM((8, HD), jnp.int32),
            pltpu.VMEM((REQ, TREE, HD), F32),
            pltpu.VMEM((REQ, TREE, HD), F32),
            pltpu.VMEM((2, BLOCK, HD), BF16),
            dma((11,)), dma((11,)), dma((2, 7)), dma((2, 7)), dma((4, REQ)), dma((4, REQ)), dma((3,)), dma((3,)),
            dma((8,)),
        ],
        compiler_params=pltpu.CompilerParams(collective_id=0, has_side_effects=True, vmem_limit_bytes=limit),
        name="project_and_gather",
    )(
        prefix_used, cache_lengths, parents, norm_gain[None, :], frequency, tokens, w_query, w_key, w_value,
        prefix_keys, prefix_values,
    )
    slots = cache_keys.shape[0]
    rows = NZ * BLOCK + slots
    o_part, stats, acc_k, acc_v = pl.pallas_call(
        attend_kernel,
        out_shape=(
            shape((NX * REQ, HD, 256), BF16),
            shape((NX, 8, 256), F32),
            shape((REQ, 8, HD), BF16),
            shape((REQ, 8, HD), BF16),
        ),
        in_specs=[smem, smem, smem] + [any_spec] * 8,
        out_specs=[any_spec, any_spec, vmem, vmem],
        scratch_shapes=[
            pltpu.VMEM((NX * REQ, 256, HD), BF16),
            pltpu.VMEM((rows + NZ * BLOCK, HD), BF16),
            pltpu.VMEM((rows, HD), BF16),
            pltpu.VMEM((HD + 16, rows), BF16),
            pltpu.VMEM((REQ, TREE, HD), BF16),
            pltpu.VMEM((REQ, TREE, HD), BF16),
            pltpu.VMEM((REQ, TREE, 256), F32),
            pltpu.VMEM((2, NZ * BLOCK, 256), F32),
            pltpu.VMEM((2, 8, 256), F32),
            pltpu.VMEM((HD + 16, 256), F32),
            pltpu.VMEM((ITEMS, HD, 256), BF16),
            pltpu.VMEM((ITEMS, 8, 256), F32),
            pltpu.VMEM((NX, 8, 256), F32),
            pltpu.SMEM((5, ITEMS), jnp.int32),
            pltpu.SMEM((ITEMS + 1,), jnp.int32),
            dma((8,)), dma((2,)),
        ],
        compiler_params=pltpu.CompilerParams(vmem_limit_bytes=limit),
        name="attend",
    )(
        used_all, cache_lengths, accepted_index, q_all.reshape(NX * REQ, 256, HD), k_all.reshape(-1, HD),
        v_all.reshape(-1, HD), new_k, new_v, anc, cache_keys, cache_values,
    )
    o_part = o_part.reshape(NX, REQ, HD, 256)
    mixed = pl.pallas_call(
        mix_kernel,
        out_shape=shape((32, 4096), BF16),
        in_specs=[any_spec] * 3,
        out_specs=vmem,
        scratch_shapes=[
            pltpu.VMEM((512, 4096), BF16),
            pltpu.VMEM((REQ, HD, 256), BF16),
            pltpu.VMEM((3, REQ, HD, 256), BF16),
            pltpu.VMEM((8, 256), F32),
            pltpu.VMEM((3, 8, 256), F32),
            pltpu.VMEM((4, 8, 256), F32),
            pltpu.VMEM((2, REQ, HD // 2, 256), BF16),
            pltpu.VMEM((TREE, 512), BF16),
            pltpu.VMEM((REQ, 2, 32, 4096), BF16),
            pltpu.VMEM((REQ, 32, 4096), BF16),
            pltpu.VMEM((32, 4096), BF16),
            pltpu.VMEM((2, 16, 4096), BF16),
            pltpu.VMEM((2, 32, 4096), BF16),
            pltpu.VMEM((2, 32, 4096), BF16),
            dma((3,)), dma((3,)), dma((6, REQ)), dma((6, REQ)), dma((REQ,)), dma((REQ,)), dma((2,)), dma((2,)),
            dma((2,)), dma((2,)), dma((3,)),
        ],
        compiler_params=pltpu.CompilerParams(collective_id=1, has_side_effects=True, vmem_limit_bytes=limit),
        name="mix",
    )(o_part, stats, w_out)
    return (mixed, acc_k, acc_v)


def solution(mesh):
    in_specs = (
        P(("batch", "tensor"), None),
        P(),
        P(None, "tensor"),
        P(None, "tensor"),
        P(None, "tensor"),
        P("tensor", None),
        P("batch", "tensor"),
        P("batch", "tensor"),
        P("batch", "tensor"),
        P("batch", "tensor"),
        P(),
        P("batch"),
        P("batch", None),
        P("batch", None),
    )
    out_specs = (
        P(("batch", "tensor"), None),
        P("batch", None, "tensor"),
        P("batch", None, "tensor"),
    )
    return jax.shard_map(body, mesh=mesh, in_specs=in_specs, out_specs=out_specs, check_vma=False)
```
